32 devices in a mesh: row: 8 (over z, core), col: 4 (over y, x).
Axes of the slice: x: 2, y: 2, z: 4, core: 2. Of those that a mesh axis runs over, the one named last changes fastest.
Arguments:
- matrix: bfloat16 [12288, 12288], P('row', 'col'), may hold values from -8 to 8, as said below
- panels: bfloat16 [2, 12288, 128], P(None, 'row'), may hold values from -1 to 1
Outputs:
- updated: bfloat16 [12288, 12288], P('row', 'col')
The draws below stay inside these ranges and needn't reach their ends.
Inputs may be any that keep to these rules, and one draw needn't show every extreme that they name: matrix is exactly symmetric.
All inputs are finite; a program needn't handle non-finite values.
Results may differ from the reference program's by a relative error of at most 0.015.
Values may be sent and summed in bfloat16 or wider, within the bound.
No kernel may reach another device: no remote copies, remote signals or barrier semaphores. Data moves between devices by JAX's collectives and lax.ppermute only.
A program may use at most 128 MiB of HBM per device.

```python
import jax
import jax.numpy as jnp
from jax import lax

B = 128
PANELS = 2
N = 12288


def draw_matrix(key, part):
    values = jnp.clip(jax.random.normal(key, (N, N), jnp.float32), -5.0, 5.0)
    return ((values + values.T) * 0.7071).astype(jnp.bfloat16)


def draw_panels(key, part):
    values = jnp.clip(jax.random.normal(jax.random.fold_in(key, 7), (PANELS, N, B), jnp.float32), -6.0, 6.0)
    return (values * (B * N) ** (-0.25)).astype(jnp.bfloat16)


def setup_inputs(seed: int = 0) -> dict:
    streams_of = jax.random.split(jax.random.key(seed), 3)
    return {
        "matrix": draw_matrix(jax.random.fold_in(streams_of[2], 71), 0),
        "panels": draw_panels(jax.random.fold_in(streams_of[2], 71), 0),
    }


def reference(matrix, panels):
    current = matrix
    for panel in range(PANELS):
        panel_v = panels[panel]
        product = jnp.dot(current, panel_v, preferred_element_type=jnp.float32)
        panel_f = panel_v.astype(jnp.float32)
        curvature = jnp.dot(panel_f.T, product, precision=lax.Precision.HIGHEST)
        w_panel = (product - 0.5 * jnp.dot(panel_f, curvature, precision=lax.Precision.HIGHEST)).astype(jnp.bfloat16)
        update = lax.dot_general(panel_v, w_panel, (((1,), (1,)), ((), ())), preferred_element_type=jnp.float32)
        update = update + lax.dot_general(w_panel, panel_v, (((1,), (1,)), ((), ())), preferred_element_type=jnp.float32)
        current = (current.astype(jnp.float32) - update).astype(jnp.bfloat16)
    return current
```

```python
import jax
import jax.numpy as jnp
from jax import lax
from jax.sharding import PartitionSpec as P

F32 = jnp.float32
BF16 = jnp.bfloat16


def dot(a, b, ca, cb):
    return lax.dot_general(a, b, (((ca,), (cb,)), ((), ())), preferred_element_type=F32)


def exact(a, b, ca=1, cb=0):
    return lax.dot_general(
        a, b, (((ca,), (cb,)), ((), ())), precision=lax.Precision.HIGHEST, preferred_element_type=F32
    )


def per_device(a_tile, panels):
    rows = lax.axis_size("row")
    cols = lax.axis_size("col")
    ratio = rows // cols
    row = lax.axis_index("row")
    col = lax.axis_index("col")
    group = row // ratio
    member = row % ratio
    n_panels, n_rows, b = panels.shape
    part = n_rows // cols
    width = n_panels * b

    def index(g, m, c):
        return (g * ratio + m) * cols + c

    def spread_pairs(t):
        return [
            (index(g, m, c), index((t - c) % cols, m, g))
            for g in range(cols)
            for m in range(ratio)
            for c in range(cols)
        ]

    def column_blocks(piece):
        pieces = [lax.ppermute(piece, ("row", "col"), spread_pairs(t)) for t in range(cols)]
        block = jnp.zeros((n_rows, width), BF16)
        for t, got in enumerate(pieces):
            block = lax.dynamic_update_slice_in_dim(block, got, (t - group) % cols * part, 0)
        full = jnp.zeros((ratio * n_rows, width), BF16)
        full = lax.dynamic_update_slice_in_dim(full, block, member * n_rows, 0)
        for o in range(1, ratio):
            pairs = [(g * ratio + m, g * ratio + (m + o) % ratio) for g in range(cols) for m in range(ratio)]
            got = lax.ppermute(block, "row", pairs)
            full = lax.dynamic_update_slice_in_dim(full, got, (member - o) % ratio * n_rows, 0)
        return full

    def shift(o):
        return [(c, (c + o) % cols) for c in range(cols)]

    def col_sum(x, wire):
        sent = x.astype(wire)
        total = x
        for o in range(1, cols):
            total = total + lax.ppermute(sent, "col", shift(o)).astype(F32)
        return total

    v_rows = jnp.concatenate([panels[p] for p in range(n_panels)], axis=1)
    v_piece = lax.dynamic_slice_in_dim(v_rows, col * part, part, 0)
    v_cols = column_blocks(v_piece)

    partial = dot(a_tile, v_cols, 1, 0)
    mine = lax.dynamic_slice_in_dim(partial, col * part, part, 0)
    sent = partial.astype(BF16)
    for o in range(1, cols):
        theirs = lax.dynamic_slice_in_dim(sent, (col + o) % cols * part, part, 0)
        mine = mine + lax.ppermute(theirs, "col", shift(o)).astype(F32)
    p_piece = mine.astype(BF16)

    s = col_sum(dot(v_cols[:, :b], v_cols[:, b:], 0, 0), F32)

    p_cols = column_blocks(p_piece)
    p_rows = jnp.zeros((n_rows, width), BF16)
    p_rows = lax.dynamic_update_slice_in_dim(p_rows, p_piece, col * part, 0)
    for o in range(1, cols):
        got = lax.ppermute(p_piece, "col", shift(o))
        p_rows = lax.dynamic_update_slice_in_dim(p_rows, got, (col - o) % cols * part, 0)

    g = col_sum(dot(v_cols, p_cols, 0, 0), BF16)
    c1 = g[:b, :b]
    g12 = g[:b, b:]
    g22 = g[b:, b:]
    k12 = exact(c1, s) - g12
    cross = exact(s, g12, 0, 0)
    c2 = g22 - cross - cross.T + exact(s, exact(c1, s), 0, 0)

    v1 = v_rows[:, :b]
    v2 = v_rows[:, b:]
    x1 = (v1.astype(F32) - exact(v2.astype(F32), s, 1, 1)).astype(BF16)
    mix = jnp.concatenate(
        [
            jnp.concatenate([-c1, k12], axis=1),
            jnp.concatenate([k12.T, -c2], axis=1),
        ],
        axis=0,
    )
    y = exact(v_rows.astype(F32), mix) + p_rows.astype(F32)
    y = y - jnp.concatenate(
        [jnp.zeros((n_rows, b), F32), exact(p_rows[:, :b].astype(F32), s)], axis=1
    )
    left = jnp.concatenate([x1, v2, y.astype(BF16)], axis=1)
    right = jnp.concatenate([p_cols, v_cols], axis=1)
    update = dot(left, right, 1, 1)
    return (a_tile.astype(F32) - update).astype(BF16)


def solution(mesh):
    in_specs = (P("row", "col"), P(None, "row", None))
    out_specs = P("row", "col")
    return jax.shard_map(
        per_device, mesh=mesh, in_specs=in_specs, out_specs=out_specs, check_vma=False
    )
```

```python
import functools

import jax
import jax.numpy as jnp
from jax import lax
from jax.experimental import pallas as pl
from jax.experimental.pallas import tpu as pltpu
from jax.sharding import PartitionSpec as P

F32 = jnp.float32
BF16 = jnp.bfloat16


def dot(a, b, ca=1, cb=0):
    return lax.dot_general(a, b, (((ca,), (cb,)), ((), ())), preferred_element_type=F32)


def exact(a, b):
    return lax.dot_general(
        a, b, (((1,), (0,)), ((), ())), precision=lax.Precision.HIGHEST, preferred_element_type=F32
    )


def halves(x):
    hi = x.astype(BF16)
    return hi, (x - hi.astype(F32)).astype(BF16)


def params(mib):
    return pltpu.CompilerParams(vmem_limit_bytes=mib * 2**20)


WHOLE = pl.BlockSpec(memory_space=pltpu.VMEM)
SCALARS = pl.BlockSpec(memory_space=pltpu.SMEM)


def rows_at(index, part):
    return pl.ds(pl.multiple_of(index * part, part), part)


def place_kernel(at_ref, *refs, groups):
    part = refs[0].shape[0]
    outs = refs[sum(groups) :]
    n = 0
    for out, size in zip(outs, groups):
        for _ in range(size):
            out[rows_at(at_ref[n], part), :] = refs[n][...]
            n += 1


def place(at, *groups):
    part, width = groups[0][0].shape
    sizes = tuple(len(pieces) for pieces in groups)
    return pl.pallas_call(
        functools.partial(place_kernel, groups=sizes),
        out_shape=[jax.ShapeDtypeStruct((size * part, width), BF16) for size in sizes],
        in_specs=[SCALARS] + [WHOLE] * sum(sizes),
        out_specs=[WHOLE] * len(sizes),
        compiler_params=params(8),
        name="place",
    )(at, *[piece for pieces in groups for piece in pieces])


def product_kernel(at_ref, a_ref, *refs, ratio, per, cols):
    blocks = refs[:ratio]
    own_ref = refs[ratio]
    sent_refs = refs[ratio + 1 : ratio + cols]
    acc_ref = refs[ratio + cols]
    i = pl.program_id(0)
    block = a_ref.shape[1]
    for m in range(ratio):
        for j in range(per):

            @pl.when(i == m * per + j)
            def _(m=m, j=j):
                value = dot(a_ref[...], blocks[m][j * block : (j + 1) * block, :])
                if m + j == 0:
                    acc_ref[...] = value
                else:
                    acc_ref[...] += value

    @pl.when(i == ratio * per - 1)
    def _():
        part = own_ref.shape[0]
        own_ref[...] = acc_ref[rows_at(at_ref[1], part), :]
        for o in range(1, cols):
            sent_refs[o - 1][...] = acc_ref[rows_at(at_ref[1 + o], part), :].astype(BF16)


def product(at, a_tile, blocks, cols, block):
    n_rows = a_tile.shape[0]
    ratio = len(blocks)
    length, width = blocks[0].shape
    part = n_rows // cols
    per = length // block

    def a_map(i, at):
        return 0, lax.rem(at[0] + i // per, ratio) * per + lax.rem(i, per)

    return pl.pallas_call(
        functools.partial(product_kernel, ratio=ratio, per=per, cols=cols),
        grid_spec=pltpu.PrefetchScalarGridSpec(
            num_scalar_prefetch=1,
            grid=(ratio * per,),
            in_specs=[pl.BlockSpec((n_rows, block), a_map)] + [WHOLE] * ratio,
            out_specs=[WHOLE] * cols,
            scratch_shapes=[pltpu.VMEM((n_rows, width), F32)],
        ),
        out_shape=[jax.ShapeDtypeStruct((part, width), F32)]
        + [jax.ShapeDtypeStruct((part, width), BF16)] * (cols - 1),
        compiler_params=params(46),
        name="product",
    )(at, a_tile, *blocks)


def small_kernel(*refs, ratio, b):
    v = refs[:ratio]
    p = refs[ratio : 2 * ratio]
    own_ref, wire_ref = refs[2 * ratio :]
    g = dot(v[0][...], p[0][...], 0, 0)
    s = dot(v[0][:, :b], v[0][:, b:], 0, 0)
    for m in range(1, ratio):
        g = g + dot(v[m][...], p[m][...], 0, 0)
        s = s + dot(v[m][:, :b], v[m][:, b:], 0, 0)
    for n, x in enumerate((g[:b, :b], g[:b, b:], g[b:, b:], s)):
        own_ref[n] = x
        wire_ref[n] = x.astype(BF16)


def small(v, p):
    b = v[0].shape[1] // 2
    return pl.pallas_call(
        functools.partial(small_kernel, ratio=len(v), b=b),
        out_shape=[jax.ShapeDtypeStruct((4, b, b), F32), jax.ShapeDtypeStruct((4, b, b), BF16)],
        in_specs=[WHOLE] * (2 * len(v)),
        out_specs=[WHOLE] * 2,
        compiler_params=params(12),
        name="small",
    )(*v, *p)


def update_kernel(at_ref, a_ref, *refs, ratio, per, cols, b):
    v = refs[:ratio]
    p = refs[ratio : 2 * ratio]
    v_rows, p_rows, own = refs[2 * ratio : 2 * ratio + 3]
    wires = refs[2 * ratio + 3 : 2 * ratio + 2 + cols]
    out_ref, left_ref = refs[2 * ratio + 2 + cols :]
    width = 2 * b
    i = pl.program_id(0)
    block = a_ref.shape[1]

    @pl.when(i == 0)
    def _():
        total = own[...]
        for wire in wires:
            total = total + wire[...].astype(F32)
        c1, g12, g22, s = total[0], total[1], total[2], total[3]
        st = s.T
        c1s = exact(c1, s)
        k12 = c1s - g12
        cross = exact(st, g12)
        c2 = g22 - cross - cross.T + exact(st, c1s)
        s_hi, s_lo = halves(s)
        st_hi, st_lo = halves(st)
        mix = jnp.concatenate(
            [jnp.concatenate([-c1, k12], axis=1), jnp.concatenate([k12.T, -c2], axis=1)], axis=0
        )
        mix_hi, mix_lo = halves(mix)
        v1 = v_rows[:, :b]
        v2 = v_rows[:, b:]
        left_ref[:, :b] = (v1.astype(F32) - (dot(v2, st_hi) + dot(v2, st_lo))).astype(BF16)
        left_ref[:, b:width] = v2
        y = dot(v_rows[...], mix_hi) + dot(v_rows[...], mix_lo) + p_rows[...].astype(F32)
        p1 = p_rows[:, :b]
        left_ref[:, width : width + b] = y[:, :b].astype(BF16)
        left_ref[:, width + b :] = (y[:, b:] - (dot(p1, s_hi) + dot(p1, s_lo))).astype(BF16)

    for m in range(ratio):
        for j in range(per):

            @pl.when(i == m * per + j)
            def _(m=m, j=j):
                rows = slice(j * block, (j + 1) * block)
                change = dot(left_ref[:, :width], p[m][rows, :], 1, 1)
                change = change + dot(left_ref[:, width:], v[m][rows, :], 1, 1)
                out_ref[...] = (a_ref[...].astype(F32) - change).astype(BF16)


def update(at, a_tile, v, p, v_rows, p_rows, own, wires, block):
    n_rows, n_cols = a_tile.shape
    ratio = len(v)
    length, width = v[0].shape
    cols = len(wires) + 1
    per = length // block

    def a_map(i, at):
        return 0, lax.rem(at[0] + i // per, ratio) * per + lax.rem(i, per)

    return pl.pallas_call(
        functools.partial(update_kernel, ratio=ratio, per=per, cols=cols, b=width // 2),
        grid_spec=pltpu.PrefetchScalarGridSpec(
            num_scalar_prefetch=1,
            grid=(ratio * per,),
            in_specs=[pl.BlockSpec((n_rows, block), a_map)] + [WHOLE] * (2 * ratio + 2 + cols),
            out_specs=pl.BlockSpec((n_rows, block), a_map),
            scratch_shapes=[pltpu.VMEM((n_rows, 2 * width), BF16)],
        ),
        out_shape=jax.ShapeDtypeStruct((n_rows, n_cols), BF16),
        compiler_params=params(46),
        name="update",
    )(at, a_tile, *v, *p, v_rows, p_rows, own, *wires)


def per_device(a_tile, panels):
    rows = lax.axis_size("row")
    cols = lax.axis_size("col")
    ratio = rows // cols
    row = lax.axis_index("row")
    col = lax.axis_index("col")
    group = lax.div(row, ratio)
    member = lax.rem(row, ratio)
    n_panels, n_rows, b = panels.shape
    part = n_rows // cols
    block = 384

    def index(g, m, c):
        return (g * ratio + m) * cols + c

    def spread(x, t):
        pairs = [
            (index(g, m, c), index((t - c) % cols, m, g))
            for g in range(cols)
            for m in range(ratio)
            for c in range(cols)
        ]
        return lax.ppermute(x, ("row", "col"), pairs)

    def share(x):
        got = [x]
        for o in range(1, ratio):
            pairs = [(g * ratio + m, g * ratio + (m - o) % ratio) for g in range(cols) for m in range(ratio)]
            got.append(lax.ppermute(x, "row", pairs))
        return got

    def across(x, o):
        return lax.ppermute(x, "col", [(c, (c + o) % cols) for c in range(cols)])

    turns = jnp.arange(cols, dtype=jnp.int32)
    v_rows = jnp.concatenate([panels[n] for n in range(n_panels)], axis=1)
    v = share(place(turns, [spread(v_rows[t * part : (t + 1) * part], t) for t in range(cols)])[0])

    at = jnp.concatenate([member[None], lax.rem(col + turns, cols)])
    mine, *sent = product(at, a_tile, v, cols, block)
    for o in range(1, cols):
        mine = mine + across(sent[o - 1], o).astype(F32)
    piece = mine.astype(BF16)

    spots = jnp.concatenate([lax.rem(turns + cols - group, cols), lax.rem(col + cols - turns, cols)])
    p_block, p_rows = place(
        spots,
        [spread(piece, t) for t in range(cols)],
        [piece] + [across(piece, o) for o in range(1, cols)],
    )
    p = share(p_block)
    own, wire = small(v, p)
    wires = [across(wire, o) for o in range(1, cols)]
    return update(at, a_tile, v, p, v_rows, p_rows, own, wires, block)


def solution(mesh):
    in_specs = (P("row", "col"), P(None, "row", None))
    out_specs = P("row", "col")
    return jax.shard_map(
        per_device, mesh=mesh, in_specs=in_specs, out_specs=out_specs, check_vma=False
    )
```

```python
import functools

import jax
import jax.numpy as jnp
from jax import lax
from jax.experimental import pallas as pl
from jax.experimental.pallas import tpu as pltpu
from jax.sharding import PartitionSpec as P

F32 = jnp.float32
BF16 = jnp.bfloat16
WHOLE = pl.BlockSpec(memory_space=pltpu.VMEM)


def params(mib):
    return pltpu.CompilerParams(vmem_limit_bytes=mib * 2**20)


def dot(a, b, ca=1, cb=0):
    return lax.dot_general(a, b, (((ca,), (cb,)), ((), ())), preferred_element_type=F32)


def exact(a, b):
    return lax.dot_general(
        a, b, (((1,), (0,)), ((), ())), precision=lax.Precision.HIGHEST, preferred_element_type=F32
    )


def halves(x):
    hi = x.astype(BF16)
    return hi, (x - hi.astype(F32)).astype(BF16)


def rows_at(index, part):
    return pl.ds(pl.multiple_of(index * part, part), part)


def sizes():
    rows = lax.axis_size("row")
    cols = lax.axis_size("col")
    return cols, rows // cols


def place():
    cols, ratio = sizes()
    row = lax.axis_index("row")
    return lax.div(row, ratio), lax.rem(row, ratio), lax.axis_index("col")


def split_kernel(panels_ref, rows_ref, *pieces):
    b = panels_ref.shape[2]
    part = pieces[0].shape[0]
    for n in range(panels_ref.shape[0]):
        rows_ref[:, n * b : (n + 1) * b] = panels_ref[n]
        for t, piece in enumerate(pieces):
            piece[:, n * b : (n + 1) * b] = panels_ref[n, t * part : (t + 1) * part, :]


def split(panels):
    cols, _ = sizes()
    n_panels, n_rows, b = panels.shape
    width = n_panels * b
    return pl.pallas_call(
        split_kernel,
        in_specs=[WHOLE],
        out_specs=[WHOLE] * (1 + cols),
        out_shape=[jax.ShapeDtypeStruct((n_rows, width), BF16)]
        + [jax.ShapeDtypeStruct((n_rows // cols, width), BF16)] * cols,
        compiler_params=params(8),
        name="split",
    )(panels)


def load_kernel(a_ref, out_ref, sem):
    copy = pltpu.make_async_copy(a_ref, out_ref, sem)
    copy.start()
    copy.wait()


def load(a_tile):
    return pl.pallas_call(
        load_kernel,
        in_specs=[pl.BlockSpec(memory_space=pl.ANY)],
        out_specs=WHOLE,
        out_shape=jax.ShapeDtypeStruct(a_tile.shape, BF16),
        scratch_shapes=[pltpu.SemaphoreType.DMA],
        compiler_params=params(44),
        cost_estimate=pl.CostEstimate(flops=0, bytes_accessed=4 * a_tile.size, transcendentals=0),
        name="load",
    )(a_tile)


def join_kernel(after_ref, *refs):
    out = refs[-1]
    part = refs[0].shape[0]
    for t, piece in enumerate(refs[:-1]):
        out[t * part : (t + 1) * part, :] = piece[...]


def join(after, pieces):
    part, width = pieces[0].shape
    return pl.pallas_call(
        join_kernel,
        out_shape=jax.ShapeDtypeStruct((len(pieces) * part, width), BF16),
        in_specs=[WHOLE] * (1 + len(pieces)),
        out_specs=WHOLE,
        compiler_params=params(8),
        name="join",
    )(after, *pieces)


def product_kernel(a_ref, *refs, cols, ratio, b):
    blocks = refs[:ratio]
    own_ref = refs[ratio]
    sent = refs[ratio + 1 :]
    _, member, col = place()
    length = blocks[0].shape[0]
    part = own_ref.shape[0]
    extra = sent[0].shape[0] - part
    s = jnp.zeros((b, b), F32)
    for block in blocks:
        s = s + dot(block[:, :b], block[:, b:], 0, 0)
    packed = jnp.concatenate([s[:extra], s[extra:]], axis=1)
    for o in range(cols):
        rows = rows_at(jnp.bitwise_xor(col, o), part)
        value = jnp.zeros((part, 2 * b), F32)
        for m in range(ratio):
            at = lax.rem(member + m, ratio)
            value = value + dot(a_ref[rows, rows_at(at, length)], blocks[m][...])
        if o == 0:
            own_ref[...] = value
        else:
            sent[o - 1][:part, :] = value.astype(BF16)
            sent[o - 1][part:, :] = packed.astype(BF16)
    sent[cols - 1][...] = packed


def product(a_tile, blocks):
    cols, ratio = sizes()
    n_rows = a_tile.shape[0]
    width = blocks[0].shape[1]
    b = width // 2
    part = n_rows // cols
    extra = b // 2
    return pl.pallas_call(
        functools.partial(product_kernel, cols=cols, ratio=ratio, b=b),
        in_specs=[WHOLE] * (1 + ratio),
        out_specs=[WHOLE] * (cols + 1),
        out_shape=[jax.ShapeDtypeStruct((part, width), F32)]
        + [jax.ShapeDtypeStruct((part + extra, width), BF16)] * (cols - 1)
        + [jax.ShapeDtypeStruct((extra, width), F32)],
        compiler_params=params(16),
        name="product",
    )(a_tile, *blocks)


def reduce_kernel(own_ref, s_ref, *refs):
    piece_ref, s_out = refs[-2:]
    part = own_ref.shape[0]
    extra = s_ref.shape[0]
    b = 2 * extra
    total = own_ref[...]
    s = s_ref[...]
    for got in refs[:-2]:
        total = total + got[:part, :].astype(F32)
        s = s + got[part:, :].astype(F32)
    piece_ref[...] = total.astype(BF16)
    s_out[:extra, :] = s[:, :b]
    s_out[extra:, :] = s[:, b:]


def reduce(own, s, got):
    b = own.shape[1] // 2
    return pl.pallas_call(
        reduce_kernel,
        in_specs=[WHOLE] * (2 + len(got)),
        out_specs=[WHOLE] * 2,
        out_shape=[jax.ShapeDtypeStruct(own.shape, BF16), jax.ShapeDtypeStruct((b, b), F32)],
        compiler_params=params(8),
        name="reduce",
    )(own, s, *got)


def arrange_kernel(*refs, cols):
    pieces = refs[:cols]
    ours = refs[cols : 2 * cols]
    block_ref, rows_ref = refs[2 * cols :]
    group, _, col = place()
    part = pieces[0].shape[0]
    for t in range(cols):
        block_ref[rows_at(lax.rem(2 * cols + group - col - t, cols), part), :] = pieces[t][...]
        rows_ref[rows_at(jnp.bitwise_xor(col, t), part), :] = ours[t][...]


def arrange(pieces, ours):
    cols, _ = sizes()
    part, width = pieces[0].shape
    shape = jax.ShapeDtypeStruct((cols * part, width), BF16)
    return pl.pallas_call(
        functools.partial(arrange_kernel, cols=cols),
        out_shape=[shape, shape],
        in_specs=[WHOLE] * (2 * cols),
        out_specs=[WHOLE] * 2,
        compiler_params=params(8),
        name="arrange",
    )(*pieces, *ours)


def gram_kernel(*refs, ratio, b):
    v = refs[:ratio]
    p = refs[ratio : 2 * ratio]
    own_ref, wire_ref = refs[2 * ratio :]
    g = dot(v[0][...], p[0][...], 0, 0)
    for m in range(1, ratio):
        g = g + dot(v[m][...], p[m][...], 0, 0)
    for n, x in enumerate((g[:b, :b], g[:b, b:], g[b:, b:])):
        own_ref[n] = x
        wire_ref[n] = x.astype(BF16)


def gram(v, p):
    b = v[0].shape[1] // 2
    return pl.pallas_call(
        functools.partial(gram_kernel, ratio=len(v), b=b),
        out_shape=[jax.ShapeDtypeStruct((3, b, b), F32), jax.ShapeDtypeStruct((3, b, b), BF16)],
        in_specs=[WHOLE] * (2 * len(v)),
        out_specs=[WHOLE] * 2,
        compiler_params=params(8),
        name="gram",
    )(*v, *p)


def update_kernel(a_ref, *refs, ratio, per, cols, b):
    v = refs[:ratio]
    p = refs[ratio : 2 * ratio]
    v_rows, p_rows, s_ref, own = refs[2 * ratio : 2 * ratio + 4]
    wires = refs[2 * ratio + 4 : 2 * ratio + 3 + cols]
    out_ref, left_ref = refs[2 * ratio + 3 + cols :]
    width = 2 * b
    i = pl.program_id(0)
    block = out_ref.shape[1]
    _, member, _ = place()

    @pl.when(i == 0)
    def _():
        total = own[...]
        for wire in wires:
            total = total + wire[...].astype(F32)
        c1, g12, g22 = total[0], total[1], total[2]
        s = s_ref[...]
        st = s.T
        k12 = exact(c1, s) - g12
        c2 = g22 + exact(st, k12) - exact(g12.T, s)
        s_hi, s_lo = halves(s)
        st_hi, st_lo = halves(st)
        mix = jnp.concatenate(
            [jnp.concatenate([-c1, k12], axis=1), jnp.concatenate([k12.T, -c2], axis=1)], axis=0
        )
        mix_hi, mix_lo = halves(mix)
        v1 = v_rows[:, :b]
        v2 = v_rows[:, b:]
        left_ref[:, :b] = (v1.astype(F32) - (dot(v2, st_hi) + dot(v2, st_lo))).astype(BF16)
        left_ref[:, b:width] = v2
        y = dot(v_rows[...], mix_hi) + dot(v_rows[...], mix_lo) + p_rows[...].astype(F32)
        p1 = p_rows[:, :b]
        left_ref[:, width : width + b] = y[:, :b].astype(BF16)
        left_ref[:, width + b :] = (y[:, b:] - (dot(p1, s_hi) + dot(p1, s_lo))).astype(BF16)

    for h in range(ratio):
        for j in range(per):
            for m in range(ratio):
                here = lax.rem(member + m, ratio) == h

                @pl.when(jnp.logical_and(i == h * per + j, here))
                def _(h=h, j=j, m=m):
                    rows = slice(j * block, (j + 1) * block)
                    start = (h * per + j) * block
                    change = dot(left_ref[:, :width], p[m][rows, :], 1, 1)
                    change = change + dot(left_ref[:, width:], v[m][rows, :], 1, 1)
                    now = a_ref[:, start : start + block].astype(F32)
                    out_ref[...] = (now - change).astype(BF16)


def update(a_tile, v, p, v_rows, p_rows, s, own, wires, block):
    n_rows, n_cols = a_tile.shape
    ratio = len(v)
    length, width = v[0].shape
    cols = len(wires) + 1
    per = length // block
    return pl.pallas_call(
        functools.partial(update_kernel, ratio=ratio, per=per, cols=cols, b=width // 2),
        grid=(ratio * per,),
        in_specs=[WHOLE] * (2 * ratio + 4 + cols),
        out_specs=pl.BlockSpec((n_rows, block), lambda i: (0, i)),
        scratch_shapes=[pltpu.VMEM((n_rows, 2 * width), BF16)],
        out_shape=jax.ShapeDtypeStruct((n_rows, n_cols), BF16),
        compiler_params=params(24),
        name="update",
    )(a_tile, *v, *p, v_rows, p_rows, s, own, *wires)


def per_device(a_tile, panels):
    cols, ratio = sizes()
    block = 512

    def index(g, m, c):
        return (g * ratio + m) * cols + c

    def spread(x, t):
        pairs = [
            (index(g, m, c), index((g + c + t) % cols, m, g))
            for g in range(cols)
            for m in range(ratio)
            for c in range(cols)
        ]
        return lax.ppermute(x, ("row", "col"), pairs)

    def share(x):
        got = [x]
        for o in range(1, ratio):
            pairs = [(g * ratio + m, g * ratio + (m - o) % ratio) for g in range(cols) for m in range(ratio)]
            got.append(lax.ppermute(x, "row", pairs))
        return got

    def across(x, o):
        return lax.ppermute(x, "col", [(c, c ^ o) for c in range(cols)])

    a_tile = load(a_tile)
    v_rows, *v_pieces = split(panels)
    v = share(join(a_tile, [spread(v_pieces[t], t) for t in range(cols)]))
    own, *sent, s_own = product(a_tile, v)
    piece, s = reduce(own, s_own, [across(sent[o - 1], o) for o in range(1, cols)])
    p_block, p_rows = arrange(
        [spread(piece, t) for t in range(cols)],
        [piece] + [across(piece, o) for o in range(1, cols)],
    )
    p = share(p_block)
    g_own, wire = gram(v, p)
    wires = [across(wire, o) for o in range(1, cols)]
    return update(a_tile, v, p, v_rows, p_rows, s, g_own, wires, block)


def solution(mesh):
    in_specs = (P("row", "col"), P(None, "row", None))
    out_specs = P("row", "col")
    return jax.shard_map(
        per_device, mesh=mesh, in_specs=in_specs, out_specs=out_specs, check_vma=False
    )
```

```python
import functools

import jax
import jax.numpy as jnp
from jax import lax
from jax.experimental import pallas as pl
from jax.experimental.pallas import tpu as pltpu
from jax.sharding import PartitionSpec as P


F32 = jnp.float32
BF16 = jnp.bfloat16
WHOLE = pl.BlockSpec(memory_space=pltpu.VMEM)


def params(mib):
    return pltpu.CompilerParams(vmem_limit_bytes=mib * 2**20)


def dot(a, b, ca=1, cb=0):
    return lax.dot_general(a, b, (((ca,), (cb,)), ((), ())), preferred_element_type=F32)


def exact(a, b):
    return lax.dot_general(
        a, b, (((1,), (0,)), ((), ())), precision=lax.Precision.HIGHEST, preferred_element_type=F32
    )


def halves(x):
    hi = x.astype(BF16)
    return hi, (x - hi.astype(F32)).astype(BF16)


def rows_at(index, part):
    return pl.ds(pl.multiple_of(index * part, part), part)


def sizes():
    rows = lax.axis_size("row")
    cols = lax.axis_size("col")
    return cols, rows // cols


def place():
    _, ratio = sizes()
    row = lax.axis_index("row")
    return lax.div(row, ratio), lax.rem(row, ratio), lax.axis_index("col")


def call(kernel, ins, outs, mib=8, **kw):
    return pl.pallas_call(
        kernel,
        in_specs=[WHOLE] * len(ins),
        out_specs=[WHOLE] * len(outs),
        out_shape=[jax.ShapeDtypeStruct(*out) for out in outs],
        compiler_params=params(mib),
        **kw,
    )(*ins)


def split_kernel(panels_ref, *pieces):
    _, _, col = place()
    for n, piece in enumerate(pieces):
        piece[...] = panels_ref[n, rows_at(col, piece.shape[0]), :]


def split(panels):
    cols, _ = sizes()
    n_panels, n_rows, b = panels.shape
    return call(split_kernel, [panels], [((n_rows // cols, b), BF16)] * n_panels)


def gate_kernel(x_ref, *refs):
    refs[-1][...] = x_ref[...]


def gate(x, *after):
    return call(gate_kernel, [x, *after], [(x.shape, BF16)])[0]


def load_kernel(a_ref, *refs):
    out_ref, sem = refs[-2:]
    copy = pltpu.make_async_copy(a_ref, out_ref, sem)
    copy.start()
    copy.wait()


def load(a_tile, *after):
    return pl.pallas_call(
        load_kernel,
        in_specs=[pl.BlockSpec(memory_space=pl.ANY)] + [WHOLE] * len(after),
        out_specs=WHOLE,
        out_shape=jax.ShapeDtypeStruct(a_tile.shape, BF16),
        scratch_shapes=[pltpu.SemaphoreType.DMA],
        compiler_params=params(44),
        name="load",
    )(a_tile, *after)


def pick_kernel(after_ref, *refs, cols):
    del after_ref
    group, _, col = place()
    for o in range(cols):
        source = jnp.bitwise_xor(group, jnp.bitwise_xor(col, o))
        for d in range(cols):

            @pl.when(source == d)
            def _(o=o, d=d):
                refs[cols + o][...] = refs[d][...]


def pick(after, pieces):
    cols = len(pieces)
    kernel = functools.partial(pick_kernel, cols=cols)
    return call(kernel, [after, *pieces], [(pieces[0].shape, BF16)] * cols)


def join_kernel(*refs, cols):
    _, _, col = place()
    out = refs[-1]
    part = refs[0].shape[0]
    for o, piece in enumerate(refs[:cols]):
        out[rows_at(jnp.bitwise_xor(col, o), part), :] = piece[...]


def join(pieces, *after):
    part, width = pieces[0].shape
    cols = len(pieces)
    kernel = functools.partial(join_kernel, cols=cols)
    return call(kernel, [*pieces, *after], [((cols * part, width), BF16)])[0]


def product_kernel(after_ref, a_ref, *refs, cols, ratio, extra):
    del after_ref
    blocks = refs[:ratio]
    others = refs[ratio : (2 if extra else 1) * ratio]
    outs = refs[ratio + len(others) :]
    _, member, col = place()
    length = blocks[0].shape[0]
    part = outs[0].shape[0]
    for o in [*range(1, cols), 0]:
        rows = rows_at(jnp.bitwise_xor(col, o), part)
        value = dot(a_ref[rows, rows_at(member, length)], blocks[0][...])
        for m in range(1, ratio):
            at = lax.rem(member + m, ratio)
            value = value + dot(a_ref[rows, rows_at(at, length)], blocks[m][...])
        outs[o][...] = value.astype(outs[o].dtype)
    if extra:
        s = dot(others[0][...], blocks[0][...], 0, 0)
        for m in range(1, ratio):
            s = s + dot(others[m][...], blocks[m][...], 0, 0)
        outs[cols][...] = s


def product(after, a_tile, blocks, others=()):
    cols, ratio = sizes()
    b = blocks[0].shape[1]
    part = a_tile.shape[0] // cols
    outs = [((part, b), F32)] + [((part, b), BF16)] * (cols - 1)
    if others:
        outs.append(((b, b), F32))
    kernel = functools.partial(product_kernel, cols=cols, ratio=ratio, extra=bool(others))
    return call(kernel, [after, a_tile, *blocks, *others], outs, 16)


def total_kernel(own_ref, after_ref, *refs, count):
    del after_ref
    value = own_ref[...]
    for got in refs[:count]:
        value = value + got[...].astype(F32)
    piece = value.astype(BF16)
    if len(refs) > count + 1:
        s_ref, piece_ref, wire_ref = refs[count:]
        part = own_ref.shape[0]
        piece_ref[...] = piece
        wire_ref[:part, :] = piece
        wire_ref[part:, :] = s_ref[...].astype(BF16)
    else:
        refs[-1][...] = piece


def total(own, got, after, *s):
    part, b = own.shape
    outs = [(own.shape, BF16)] + [((part + b, b), BF16)] * len(s)
    kernel = functools.partial(total_kernel, count=len(got))
    return call(kernel, [own, after, *got, *s], outs)


def gram_kernel(*refs, ratio):
    v1, v2, p1, p2 = (refs[n * ratio : (n + 1) * ratio] for n in range(4))
    own_ref, wire_ref = refs[4 * ratio :]
    for n, (left, right) in enumerate(((v1, p1), (v1, p2), (v2, p2))):
        g = dot(left[0][...], right[0][...], 0, 0)
        for m in range(1, ratio):
            g = g + dot(left[m][...], right[m][...], 0, 0)
        own_ref[n] = g
        wire_ref[n] = g.astype(BF16)


def gram(v1, v2, p1, p2):
    b = v1[0].shape[1]
    outs = [((3, b, b), F32), ((3, b, b), BF16)]
    return call(functools.partial(gram_kernel, ratio=len(v1)), [*v1, *v2, *p1, *p2], outs)


def pack_kernel(after_ref, panels_ref, s_ref, *refs, ratio, cols, b):
    del after_ref
    parts = [refs[n * ratio : (n + 1) * ratio] for n in range(4)]
    firsts = refs[4 * ratio : 4 * ratio + cols]
    seconds = refs[4 * ratio + cols : 4 * ratio + 2 * cols]
    rights = refs[4 * ratio + 2 * cols : 5 * ratio + 2 * cols]
    x_ref, y_ref, s_out = refs[5 * ratio + 2 * cols :]
    _, _, col = place()
    for m in range(ratio):
        for n in range(4):
            rights[m][:, n * b : (n + 1) * b] = parts[n][m][...]
    part = seconds[0].shape[0]
    s = s_ref[...]
    for wire in firsts[1:]:
        s = s + wire[part:, :].astype(F32)
    s_out[...] = s
    s_hi, s_lo = halves(s)
    st_hi, st_lo = halves(s.T)
    v1 = panels_ref[0]
    v2 = panels_ref[1]
    x_ref[:, :b] = (v1.astype(F32) - (dot(v2, st_hi) + dot(v2, st_lo))).astype(BF16)
    x_ref[:, b:] = v2
    for o in range(cols):
        rows = rows_at(jnp.bitwise_xor(col, o), part)
        p1 = firsts[o][:part, :]
        y_ref[rows, :b] = p1.astype(F32)
        y_ref[rows, b:] = seconds[o][...].astype(F32) - (dot(p1, s_hi) + dot(p1, s_lo))


def pack(after, panels, s, p1, p2, v1, v2, firsts, seconds):
    _, n_rows, b = panels.shape
    ratio = len(v1)
    cols = len(firsts)
    outs = [((n_rows, 4 * b), BF16)] * ratio + [((n_rows, 2 * b), BF16), ((n_rows, 2 * b), F32), ((b, b), F32)]
    kernel = functools.partial(pack_kernel, ratio=ratio, cols=cols, b=b)
    ins = [after, panels, s, *p1, *p2, *v1, *v2, *firsts, *seconds]
    out = call(kernel, ins, outs, 16)
    return out[:ratio], *out[ratio:]


def update_kernel(a_ref, panels_ref, x_ref, y_ref, s_ref, own, *refs, ratio, per, cols, b):
    wires = refs[: cols - 1]
    rights = refs[cols - 1 : cols - 1 + ratio]
    out_ref, left_ref, slots, sems = refs[cols - 1 + ratio :]
    width = 2 * b
    block = slots.shape[2]
    _, member, _ = place()

    total = own[...]
    for wire in wires:
        total = total + wire[...].astype(F32)
    c1, g12, g22 = total[0], total[1], total[2]
    s = s_ref[...]
    k12 = exact(c1, s) - g12
    c2 = g22 + exact(s.T, k12) - exact(g12.T, s)
    top_hi, top_lo = halves(jnp.concatenate([-c1, k12], axis=1))
    low_hi, low_lo = halves(jnp.concatenate([k12.T, -c2], axis=1))
    v1 = panels_ref[0]
    v2 = panels_ref[1]
    y = y_ref[...] + (dot(v1, top_hi) + dot(v2, low_hi)) + (dot(v1, top_lo) + dot(v2, low_lo))
    left_ref[:, :width] = x_ref[...]
    left_ref[:, width:] = y.astype(BF16)

    copies = []
    for m in range(ratio):
        for j in range(per):
            n = m * per + j
            start = pl.multiple_of((lax.rem(member + m, ratio) * per + j) * block, block)
            if n >= 2:
                copies[n - 2].wait()
            change = dot(left_ref[...], rights[m][j * block : (j + 1) * block, :], 1, 1)
            now = a_ref[:, pl.ds(start, block)].astype(F32)
            slots[n % 2] = (now - change).astype(BF16)
            copies.append(
                pltpu.make_async_copy(slots.at[n % 2], out_ref.at[:, pl.ds(start, block)], sems.at[n % 2])
            )
            copies[n].start()
    for copy in copies[-2:]:
        copy.wait()


def update(a_tile, panels, x, y, s, own, wires, rights, block):
    n_rows, n_cols = a_tile.shape
    ratio = len(rights)
    length, width = rights[0].shape
    cols = len(wires) + 1
    per = length // block
    return pl.pallas_call(
        functools.partial(update_kernel, ratio=ratio, per=per, cols=cols, b=width // 4),
        in_specs=[WHOLE] * (5 + cols + ratio),
        out_specs=pl.BlockSpec(memory_space=pl.ANY),
        scratch_shapes=[
            pltpu.VMEM((n_rows, width), BF16),
            pltpu.VMEM((2, n_rows, block), BF16),
            pltpu.SemaphoreType.DMA((2,)),
        ],
        out_shape=jax.ShapeDtypeStruct((n_rows, n_cols), BF16),
        compiler_params=params(24),
        name="update",
    )(a_tile, panels, x, y, s, own, *wires, *rights)


def body(a_tile, panels):
    cols, ratio = sizes()

    def across(x, o):
        return lax.ppermute(x, "col", [(c, c ^ o) for c in range(cols)])

    def along(x, d):
        pairs = [(g * ratio + m, (g ^ d) * ratio + m) for g in range(cols) for m in range(ratio)]
        return lax.ppermute(x, "row", pairs)

    def share(x):
        got = [x]
        for o in range(1, ratio):
            pairs = [(g * ratio + m, g * ratio + (m - o) % ratio) for g in range(cols) for m in range(ratio)]
            got.append(lax.ppermute(x, "row", pairs))
        return got

    def gather(x):
        pieces = {0: x}
        step = cols // 2
        while step:
            for d in list(pieces):
                pieces[d | step] = along(pieces[d], step)
            step //= 2
        return [pieces[d] for d in range(cols)]

    def trade(kept, *sent):
        return [kept] + [across(sent[o - 1], o) for o in range(1, cols)]

    piece1, piece2 = split(panels)
    tile = load(a_tile, piece1)
    far1 = gather(piece1)
    piece2 = gate(piece2, far1[cols // 2])
    far2 = gather(piece2)
    picked1 = pick(piece2, far1)
    block1 = join(trade(*picked1), tile)
    v1 = share(block1)
    picked2 = pick(block1, far2)
    own1, *sent1 = product(picked2[0], tile, v1)
    block2 = join(trade(*picked2), own1)
    v2 = share(block2)
    *out2, s_own = product(block2, tile, v2, v1)
    own2, *sent2 = out2

    piece1, wire1 = total(own1, trade(own1, *sent1)[1:], own2, s_own)
    far1 = gather(piece1)
    firsts = trade(*[wire1] * cols)
    piece2 = total(own2, trade(own2, *sent2)[1:], piece1)[0]
    far2 = gather(piece2)
    seconds = trade(*[piece2] * cols)
    picked1 = pick(piece2, far1)
    picked2 = pick(picked1[0], far2)
    block1 = join(trade(*picked1), picked2[0])
    p1 = share(block1)
    block2 = join(trade(*picked2), block1)
    p2 = share(block2)
    own, gwire = gram(v1, v2, p1, p2)
    gwires = trade(*[gwire] * cols)[1:]
    rights, x, y, s = pack(own, panels, s_own, p1, p2, v1, v2, firsts, seconds)
    return update(tile, panels, x, y, s, own, gwires, rights, 512)


def solution(mesh):
    in_specs = (P("row", "col"), P(None, "row", None))
    out_specs = P("row", "col")
    return jax.shard_map(body, mesh=mesh, in_specs=in_specs, out_specs=out_specs, check_vma=False)
```
